512 devices in a mesh: tok: 32 (over y, x), layer: 16 (over z, core).
Axes of the slice: x: 4, y: 8, z: 8, core: 2. Of those that a mesh axis runs over, the one named last changes fastest.
Arguments:
- activations: bfloat16 [16, 14336, 5120], P(None, ('tok', 'layer')), may hold values from -9 to 9
- pos_weight: bfloat16 [16, 48, 5120], P('layer', None, 'tok'), may hold values from -1 to 1
- depth_weight: bfloat16 [16, 128, 5120], P('layer', None, 'tok'), may hold values from -0.01953125 to 0.01953125
- tags: int32 [14336], P(('tok', 'layer')), may hold values from 0 to 47
- depths: int32 [14336], P(('tok', 'layer')), may hold values from 2 to 14
- counts: int32 [512], P(('tok', 'layer')), may hold values from 1 to 28, 8960 in all
Outputs:
- pos_grad: float32 [16, 48, 5120], P('layer', None, 'tok')
- depth_grad: float32 [16, 128, 5120], P('layer', None, 'tok')
The draws below stay inside these ranges and needn't reach their ends.
Inputs may be any that keep to these rules, and one draw needn't show every extreme that they name: counts[d] is the number of live slots among device d's 28 slots, which are its first ones; the largest count equals 28.
All inputs are finite; a program needn't handle non-finite values.
Results may differ from the reference program's by a relative error of at most 0.0042.
Values may be sent and summed in bfloat16 or wider, within the bound.
A program may use at most 64 MiB of HBM per device.

```python
import math
import jax
import jax.numpy as jnp
import numpy as np
from jax import lax

D = 5120
TAGS = 48
RANK = 128
TOK_DEV = 28
LAYERS = 16
TOKENS = 14336
DEVICES = 512


def probe_table(key):
    base = jax.random.normal(jax.random.fold_in(key, 11), (LAYERS, TAGS, D), jnp.float32)
    table = jnp.clip(base, -6.0, 6.0) / jnp.sqrt(jnp.float32(D))
    return table


def draw_pos_weight(key, part):
    return probe_table(key).astype(jnp.bfloat16)


def draw_activations(key, part):
    noise = jax.random.normal(jax.random.fold_in(key, 12), (LAYERS, TOKENS, D), jnp.float32)
    rows = jnp.clip(noise, -6.0, 6.0)
    return rows.astype(jnp.bfloat16)


def plant(entries, own_key, low, high):
    shape = entries.shape
    place = [jax.random.randint(jax.random.fold_in(own_key, axis), (), 0, shape[axis]) for axis in range(len(shape))]
    entries = entries.at[tuple(place)].set(low)
    longest = shape.index(max(shape))
    place[longest] = (place[longest] + 1) % shape[longest]
    return entries.at[tuple(place)].set(high)


def block_scale(key, dims, cuts, least, high):
    loudness = 1.0
    for axis_at, shards_of in cuts:
        heights = jax.random.uniform(jax.random.fold_in(jax.random.fold_in(key, 6), axis_at), (shards_of,), jnp.float32, least / len(cuts), high / len(cuts))
        loudness = loudness * jnp.repeat(jnp.exp(heights), dims[axis_at] // shards_of).reshape((-1,) + (1,) * (len(dims) - 1 - axis_at))
    return loudness


def split_up(count, total, most, lean):
    weights = [(1 << 20) // math.isqrt(standing ** lean) + 1 for standing in range(2, count + 1)]
    surplus, holding = total - most - (count - 1), [1] * (count - 1)
    while surplus > 0:
        candidates = [i for i in range(count - 1) if holding[i] < most]
        mass, remaining = sum([weights[i] for i in candidates]), surplus
        for i in candidates:
            extra = min(most - holding[i], max(1, remaining * weights[i] // mass), surplus)
            holding[i] = holding[i] + extra
            surplus = surplus - extra
    return np.array([most] + holding)


def ragged(own_key, number_of, total, limit, lean):
    if number_of == 2:
        one = jax.random.randint(own_key, (), max(1, total - limit), min(limit, total - 1) + 1)
        return jnp.stack([one, total - one])
    tallies = jnp.asarray(split_up(number_of, total, limit, lean), jnp.int32)
    couples = (number_of - 1) // 2
    giver, receiver = tallies[1:1 + 2 * couples:2], tallies[2:2 + 2 * couples:2]
    slack = jnp.minimum(giver - 1, limit - receiver)
    passed = jax.random.randint(jax.random.fold_in(own_key, 1), (couples,), 0, 1 << 20) % (slack + 1)
    tallies = tallies.at[1:1 + 2 * couples:2].set(giver - passed).at[2:2 + 2 * couples:2].set(receiver + passed)
    return tallies[jax.random.permutation(jax.random.fold_in(own_key, 2), number_of)]


def centred(rng, extent, width, bound, cuts=(), held_as=jnp.bfloat16):
    result = jax.random.normal(rng, extent, jnp.float32) * width
    if len(cuts) > 0:
        result = block_scale(rng, extent, cuts, -0.22, 0.18) * result
    return jnp.clip(result, min=-bound, max=bound).astype(held_as)


def setup_inputs(seed: int = 0) -> dict:
    splits = jax.random.split(jax.random.key(seed), 7)
    activations = draw_activations(jax.random.fold_in(splits[6], 71), 0)
    pos_weight = draw_pos_weight(jax.random.fold_in(splits[6], 71), 0)
    depth_weight = centred(splits[2], (LAYERS, RANK, D), (16 * D) ** -0.5, 0.01953125, ((0, 16), (2, 32)))
    tags = plant(jax.random.randint(splits[3], (TOKENS,), 0, TAGS), jax.random.fold_in(splits[3], 1), 0, TAGS - 1).astype(jnp.int32)
    depths = plant(jax.random.randint(splits[4], (TOKENS,), 2, 15), jax.random.fold_in(splits[4], 1), 2, 14).astype(jnp.int32)
    counts = ragged(splits[5], DEVICES, DEVICES * TOK_DEV * 5 // 8, TOK_DEV, 2).astype(jnp.int32)
    return {"activations": activations, "pos_weight": pos_weight, "depth_weight": depth_weight, "tags": tags, "depths": depths, "counts": counts}


def layer_grads(layer_rows, pos_layer, depth_layer, tags, depths, counts):
    logits = jnp.dot(layer_rows, pos_layer.T, preferred_element_type=jnp.float32)
    hidden = jnp.dot(layer_rows, depth_layer.T, preferred_element_type=jnp.float32)
    slot_index = jnp.arange(TOKENS, dtype=jnp.int32)
    position = slot_index % TOK_DEV
    block_index = slot_index // TOK_DEV
    block_count = counts[block_index]
    live = position < block_count
    token_scale = jnp.where(live, 1.0 / block_count.astype(jnp.float32), jnp.float32(0.0))
    top = jnp.max(logits, axis=1, keepdims=True)
    expo = jnp.exp(logits - top)
    probabilities = expo / jnp.sum(expo, axis=1, keepdims=True)
    onehot = (tags[:, None] == jnp.arange(TAGS, dtype=jnp.int32)[None, :]).astype(jnp.float32)
    g_pos = (probabilities - onehot) * token_scale[:, None]
    predicted = jnp.sum(hidden * hidden, axis=1)
    residual = predicted - depths.astype(jnp.float32)
    g_depth = hidden * (residual * token_scale)[:, None]
    joined = jnp.concatenate([g_pos, g_depth], axis=1).astype(jnp.bfloat16)
    grad = lax.dot_general(joined, layer_rows, (((0,), (0,)), ((), ())), preferred_element_type=jnp.float32)
    return grad[:TAGS], grad[TAGS:]


def reference(activations, pos_weight, depth_weight, tags, depths, counts):
    def one_layer(items):
        return layer_grads(items[0], items[1], items[2], tags, depths, counts)

    pos_grad, depth_grad = lax.map(one_layer, (activations, pos_weight, depth_weight))
    return pos_grad, depth_grad
```

```python
import jax
import jax.numpy as jnp
from jax import lax
from jax.experimental import pallas as pl
from jax.experimental.pallas import tpu as pltpu
from jax.sharding import PartitionSpec as P

MESH = pl.DeviceIdType.MESH
F32, BF16 = jnp.float32, jnp.bfloat16

D, TAGS, RANK, SLOTS = 5120, 48, 128, 28
K = TAGS + RANK
PAD = 32
NX, NY, NQ, NR = 4, 8, 4, 4
GROUP = NX * NR
CHUNKS, WIDE = 4, D // 4
OWN = D // NY
SUBS = ((0, 96), (96, 80))
PARTS = ((0, 24), (24, 4))
PARTNERS = tuple((dx, dr) for dr in range(NR) for dx in (1, 3, 2, 0) if (dx, dr) != (0, 0))


def place():
    tok, lay = lax.axis_index("tok"), lax.axis_index("layer")
    return lax.div(tok, NX), lax.rem(tok, NX), lax.div(lay, NR), lax.rem(lay, NR)


def dev(y, x, q, r):
    return {"tok": y * NX + x, "layer": q * NR + r}


def wrap(v, n):
    return lax.rem(v + n, n)


def send(src, dst, ssem, rsem, device):
    return pltpu.make_async_remote_copy(
        src_ref=src, dst_ref=dst, send_sem=ssem, recv_sem=rsem, device_id=device, device_id_type=MESH
    )


def kernel(
    x_hbm, w_ref, meta_ref, pos_out, dep_out,
    xin, outbox, rows, wwin, wx, wf, meta_own, meta_in, acc, g_ref,
    right_out, right_in, left_out, left_in, mine, r2_in, r3_in,
    load_sem, act_s, act_r, w_s, w_r, wr_s, wr_r, wl_s, wl_r, meta_s, meta_r,
    rr_s, rr_r, rl_s, rl_r, r2_s, r2_r, r3_s, r3_r,
):
    y, x, q, r = place()
    me = x * NR + r
    here = dev(y, x, q, r)
    up, down = dev(wrap(y + 1, NY), x, q, r), dev(wrap(y - 1, NY), x, q, r)

    def partner(dx, dr):
        px, pr = wrap(x + dx, NX), wrap(r + dr, NR)
        return px * NR + pr, dev(y, px, q, pr)

    loads = [
        pltpu.make_async_copy(x_hbm.at[:, pl.ds(k * WIDE, WIDE)], xin.at[k], load_sem.at[k])
        for k in range(CHUNKS)
    ]
    for c in loads:
        c.start()
    rows[:, 16:PAD, :] = jnp.zeros((GROUP, PAD - 16, D), BF16)
    home = x == q

    barrier = pltpu.get_barrier_semaphore()

    def greet(device):
        pl.semaphore_signal(barrier, inc=1, device_id=device, device_id_type=MESH)

    for dx, dr in PARTNERS:
        greet(partner(dx, dr)[1])
    for d in range(1, NQ):
        greet(dev(y, x, wrap(q + d, NQ), r))
    greet(up)
    greet(down)
    for sx in range(NX):
        @pl.when(jnp.logical_or(sx != x, q != x))
        def _():
            greet(dev(y, sx, x, r))

    wwin[...] = pltpu.roll(w_ref[...].astype(F32), 32 * x, 1).astype(BF16)
    meta_own[...] = pltpu.roll(meta_ref[...], 32 * r, 1)
    pl.semaphore_wait(barrier, len(PARTNERS) + NQ - 1 + 2 + NX - home.astype(jnp.int32))

    def w_send(q2):
        return send(wwin, wx.at[x], w_s.at[q2], w_r.at[x], dev(y, q, q2, r))

    for q2 in range(NQ):
        @pl.when(jnp.logical_not(jnp.logical_and(home, q2 == q)))
        def _():
            w_send(q2).start()

    @pl.when(home)
    def _():
        wx[x] = wwin[...]

    def meta_send(i, dx, dr):
        slot, device = partner(dx, dr)
        return send(meta_own, meta_in.at[me], meta_s.at[i], meta_r.at[me], device)

    for i, (dx, dr) in enumerate(PARTNERS):
        meta_send(i, dx, dr).start()
    meta_in[me] = meta_own[...]

    ri = lax.broadcasted_iota(jnp.int32, (256, 256), 0)
    ci = lax.broadcasted_iota(jnp.int32, (256, 256), 1)
    turn = jnp.where(ci == lax.rem(ri, 16) * 16 + lax.div(ri, 16), 1.0, 0.0).astype(BF16)

    def act_send(k, i, j):
        dx, dr = PARTNERS[i]
        slot, device = partner(dx, dr)
        lo, n = PARTS[j]
        return send(
            outbox.at[k, slot, pl.ds(lo, n)],
            rows.at[me, pl.ds(lo, n), pl.ds(k * WIDE, WIDE)],
            act_s.at[k, i, j], act_r.at[k, me, j], device,
        )

    def turn_and_send(k):
        loads[k].wait()

        @pl.loop(0, WIDE // 256)
        def _(b):
            cols = pl.ds(pl.multiple_of(b * 256, 256), 256)
            first = jnp.dot(turn, xin[k, 0:256, cols], preferred_element_type=F32)
            outbox[k, :, 0:16, cols] = first.astype(BF16).reshape(16, 16, 256)
            last = jnp.dot(turn[:, 0:192], xin[k, 256:448, cols], preferred_element_type=F32)
            outbox[k, :, 16:32, cols] = last.astype(BF16).reshape(16, 16, 256)

        for i in range(len(PARTNERS)):
            for j in range(2):
                act_send(k, i, j).start()
        rows[me, :, k * WIDE:(k + 1) * WIDE] = outbox[k, me]

    for k in range(CHUNKS):
        turn_and_send(k)

    for sx in range(NX):
        @pl.when(jnp.logical_or(sx != x, q != x))
        def _():
            send(wwin, wx.at[sx], w_s.at[0], w_r.at[sx], dev(y, sx, x, r)).wait_recv()
    for t in range(5):
        part = None
        for sx in (t - 1, t):
            if 0 <= sx < NX:
                lo = 128 * (t - sx)
                v = wx[sx, :, lo:lo + 128].astype(F32)
                part = v if part is None else part + v
        wf[y, :, 128 * t:128 * (t + 1)] = part.astype(BF16)

    def ring(s, way):
        at = wrap(y - s, NY) if way > 0 else wrap(y + s, NY)
        ss, rs = (wr_s, wr_r) if way > 0 else (wl_s, wl_r)
        return send(wf.at[at], wf.at[at], ss.at[s], rs.at[s], up if way > 0 else down)

    for s in range(4):
        for way, steps in ((1, 4), (-1, 3)):
            if s < steps:
                if s > 0:
                    ring(s - 1, way).wait_recv()
                ring(s, way).start()
    ring(3, 1).wait_recv()
    ring(2, -1).wait_recv()

    acc[...] = jnp.zeros_like(acc)

    @pl.loop(0, CHUNKS)
    def _(k):
        for i, (dx, dr) in enumerate(PARTNERS):
            slot, device = partner(dx, dr)
            for j, (lo, n) in enumerate(PARTS):
                send(
                    outbox.at[0, slot, pl.ds(lo, n)],
                    rows.at[slot, pl.ds(lo, n), pl.ds(pl.multiple_of(k * WIDE, WIDE), WIDE)],
                    act_s.at[k, i, j], act_r.at[k, slot, j], device,
                ).wait_recv()
        for h in range(2):
            cols = pl.ds(pl.multiple_of(k * WIDE + h * OWN, 128), OWN)
            acc[...] += lax.dot_general(
                wf[2 * k + h], rows[:, :, cols].reshape(GROUP * PAD, OWN),
                (((1,), (1,)), ((), ())), preferred_element_type=F32,
            )

    for i, (dx, dr) in enumerate(PARTNERS):
        slot, device = partner(dx, dr)
        send(meta_own, meta_in.at[slot], meta_s.at[i], meta_r.at[slot], device).wait_recv()
    facts = jnp.concatenate(
        [sum(meta_in[NR * sx + sr] for sr in range(NR)) for sx in range(NX)], axis=1
    )
    tags, depths, scale = facts[0:1], facts[1:2], facts[2:3]
    logits, hidden = acc[0:TAGS], acc[TAGS:K]
    expo = jnp.exp(logits - jnp.max(logits, axis=0, keepdims=True))
    probs = expo / jnp.sum(expo, axis=0, keepdims=True)
    names = lax.broadcasted_iota(jnp.int32, (TAGS, GROUP * PAD), 0).astype(F32)
    onehot = jnp.where(names == tags, 1.0, 0.0)
    g_ref[0:TAGS] = ((probs - onehot) * scale).astype(BF16)
    predicted = jnp.sum(hidden * hidden, axis=0, keepdims=True)
    g_ref[TAGS:K] = (hidden * ((predicted - depths) * scale)).astype(BF16)

    def block(at, sub):
        lo, n = sub
        cols = pl.ds(pl.multiple_of(at * OWN, 128), OWN)
        return jnp.dot(
            g_ref[lo:lo + n], rows[:, :, cols].reshape(GROUP * PAD, OWN), preferred_element_type=F32
        )

    def hop(s, u, way):
        lo, n = SUBS[u]
        out, inn, ss, rs = (right_out, right_in, rr_s, rr_r) if way > 0 else (left_out, left_in, rl_s, rl_r)
        return send(
            out.at[s, pl.ds(lo, n)], inn.at[s, pl.ds(lo, n)], ss.at[s, u], rs.at[s, u],
            up if way > 0 else down,
        )

    for s in range(4):
        for u, (lo, n) in enumerate(SUBS):
            for way, steps in ((1, 4), (-1, 3)):
                if s >= steps:
                    continue
                out, inn = (right_out, right_in) if way > 0 else (left_out, left_in)
                at = wrap(y + 4 - s, NY) if way > 0 else wrap(y - 3 + s, NY)
                value = block(at, (lo, n))
                if s > 0:
                    hop(s - 1, u, way).wait_recv()
                    value = value + inn[s - 1, lo:lo + n].astype(F32)
                out[s, lo:lo + n] = value.astype(BF16)
                hop(s, u, way).start()
    for u, (lo, n) in enumerate(SUBS):
        value = block(y, (lo, n))
        hop(2, u, -1).wait_recv()
        value = value + left_in[2, lo:lo + n].astype(F32)
        hop(3, u, 1).wait_recv()
        mine[lo:lo + n] = (value + right_in[3, lo:lo + n].astype(F32)).astype(BF16)

    def r2(dx):
        px = wrap(x + dx, NX)
        return send(
            mine.at[:, pl.ds(pl.multiple_of(128 * px, 128), 256)], r2_in.at[x],
            r2_s.at[dx], r2_r.at[x], dev(y, px, q, r),
        )

    for dx in (1, 3, 2):
        r2(dx).start()
    r2_in[x] = mine[:, pl.ds(pl.multiple_of(128 * x, 128), 256)]

    def r3(dq):
        pq = wrap(q + dq, NQ)
        return send(r2_in.at[pq], r3_in.at[q], r3_s.at[dq], r3_r.at[q], dev(y, x, pq, r))

    def r2_arrived(sx):
        @pl.when(sx != x)
        def _():
            send(mine.at[:, pl.ds(0, 256)], r2_in.at[sx], r2_s.at[0], r2_r.at[sx], dev(y, sx, q, r)).wait_recv()

    for dq in (1, 3, 2):
        r2_arrived(wrap(q + dq, NQ))
        r3(dq).start()
    r2_arrived(q)
    total = r2_in[q].astype(F32)
    for dq in (1, 3, 2):
        sq = wrap(q + dq, NQ)
        send(mine.at[:, pl.ds(0, 256)], r3_in.at[sq], r3_s.at[0], r3_r.at[sq], dev(y, x, sq, r)).wait_recv()
        total = total + r3_in[sq].astype(F32)
    total = pltpu.roll(total, lax.rem(256 - 32 * x, 256), 1)
    pos_out[...] = total[0:TAGS, 0:160]
    dep_out[...] = total[TAGS:K].T[0:160]

    for q2 in range(NQ):
        @pl.when(jnp.logical_not(jnp.logical_and(home, q2 == q)))
        def _():
            w_send(q2).wait_send()
    for i, (dx, dr) in enumerate(PARTNERS):
        meta_send(i, dx, dr).wait_send()
        for k in range(CHUNKS):
            for j in range(2):
                act_send(k, i, j).wait_send()
    for s in range(4):
        for way, steps in ((1, 4), (-1, 3)):
            if s < steps:
                ring(s, way).wait_send()
                for u in range(2):
                    hop(s, u, way).wait_send()
    for d in (1, 3, 2):
        r2(d).wait_send()
        r3(d).wait_send()


def local(activations, pos_weight, depth_weight, tags, depths, counts):
    acts = jnp.transpose(activations, (1, 0, 2)).reshape(SLOTS * 16, D)
    probes = jnp.pad(jnp.concatenate([pos_weight[0], depth_weight[0]], axis=0), ((0, 0), (0, 96)))
    lane = jnp.arange(128, dtype=jnp.int32)
    count = counts[0]
    scale = jnp.where(lane < count, 1.0 / count.astype(F32), F32(0.0))
    wide = lambda v: jnp.pad(v.astype(F32), (0, 128 - SLOTS))
    facts = jnp.pad(jnp.stack([wide(tags), wide(depths), scale]), ((0, 5), (0, 0)))
    dma, vm = pltpu.SemaphoreType.DMA, pltpu.VMEM
    pos, dep = pl.pallas_call(
        kernel,
        out_shape=(jax.ShapeDtypeStruct((TAGS, 160), F32), jax.ShapeDtypeStruct((160, RANK), F32)),
        in_specs=[pl.BlockSpec(memory_space=pl.ANY), pl.BlockSpec(memory_space=vm), pl.BlockSpec(memory_space=vm)],
        out_specs=(pl.BlockSpec(memory_space=vm), pl.BlockSpec(memory_space=vm)),
        scratch_shapes=[
            vm((CHUNKS, SLOTS * 16, WIDE), BF16), vm((CHUNKS, 16, PAD, WIDE), BF16), vm((GROUP, PAD, D), BF16),
            vm((K, 256), BF16), vm((NX, K, 256), BF16), vm((NY, K, OWN), BF16),
            vm((8, 128), F32), vm((GROUP, 8, 128), F32), vm((K, GROUP * PAD), F32), vm((K, GROUP * PAD), BF16),
            vm((4, K, OWN), BF16), vm((4, K, OWN), BF16), vm((3, K, OWN), BF16), vm((3, K, OWN), BF16),
            vm((K, OWN), BF16), vm((NX, K, 256), BF16), vm((NQ, K, 256), BF16),
            dma((CHUNKS,)), dma((CHUNKS, 15, 2)), dma((CHUNKS, GROUP, 2)), dma((NQ,)), dma((NX,)),
            dma((4,)), dma((4,)), dma((3,)), dma((3,)), dma((15,)), dma((GROUP,)),
            dma((4, 2)), dma((4, 2)), dma((3, 2)), dma((3, 2)), dma((4,)), dma((NX,)), dma((4,)), dma((NQ,)),
        ],
        compiler_params=pltpu.CompilerParams(
            collective_id=0, has_side_effects=True, vmem_limit_bytes=56 * 1024 * 1024
        ),
    )(acts, probes, facts)
    return pos[None], dep.T[None]


def solution(mesh):
    in_specs = (
        P(None, ("tok", "layer"), None),
        P("layer", None, "tok"),
        P("layer", None, "tok"),
        P(("tok", "layer")),
        P(("tok", "layer")),
        P(("tok", "layer")),
    )
    out_specs = (P("layer", None, "tok"), P("layer", None, "tok"))
    return jax.shard_map(local, mesh=mesh, in_specs=in_specs, out_specs=out_specs, check_vma=False)
```

```python
import jax
import jax.numpy as jnp
from jax import lax
from jax.experimental import pallas as pl
from jax.experimental.pallas import tpu as pltpu
from jax.sharding import PartitionSpec as P

MESH = pl.DeviceIdType.MESH
F32, BF16 = jnp.float32, jnp.bfloat16

D, TAGS, RANK, SLOTS = 5120, 48, 128, 28
K = TAGS + RANK
PAD = 32
NX, NY, NQ, NR = 4, 8, 4, 4
GROUP = NX * NR
CHUNKS, WIDE = 4, D // 4
OWN = D // NY
SUBS = ((0, 48), (48, 48), (96, 48), (144, 32))
PARTS = ((0, 24), (24, 4))
PARTNERS = tuple(
    (oc, db, dx) for oc in (0, 1) for db in (0, 1) for dx in (1, 3, 2, 0) if (oc, db, dx) != (0, 0, 0)
)


def wrap(v, n):
    return lax.rem(v + n, n)


def at_z(y, x, z, c):
    return {"tok": y * NX + x, "layer": 2 * z + c}


def pair_of(z, c):
    shifted = wrap(z - c, 8)
    return lax.div(shifted, 2), lax.rem(shifted, 2)


def in_pair(q, b, c):
    return lax.rem(2 * q + b + c, 8)


def send(src, dst, ssem, rsem, device):
    return pltpu.make_async_remote_copy(
        src_ref=src, dst_ref=dst, send_sem=ssem, recv_sem=rsem, device_id=device, device_id_type=MESH
    )


def kernel(
    x_hbm, wp_ref, wd_ref, tags_ref, depths_ref, counts_ref, pos_out, dep_out,
    xin, outbox, rows, wide, wwin, wxp, wxd, wf, meta_own, meta_in, acc, g_ref,
    right_out, right_in, left_out, left_in, mine, r2_in, r3_in,
    load_sem, act_s, act_r, wp_s, wp_r, wd_s, wd_r, wr_s, wr_r, wl_s, wl_r, meta_s, meta_r,
    rr_s, rr_r, rl_s, rl_r, r2_s, r2_r, r3_s, r3_r,
):
    tok, lay = lax.axis_index("tok"), lax.axis_index("layer")
    y, x, z, c = lax.div(tok, NX), lax.rem(tok, NX), lax.div(lay, 2), lax.rem(lay, 2)
    q, b = pair_of(z, c)
    me = x * NR + 2 * b + c
    zi, zb = lax.div(z, 2), lax.rem(z, 2)
    up, down = at_z(wrap(y + 1, NY), x, z, c), at_z(wrap(y - 1, NY), x, z, c)

    def target(i):
        oc, db, dx = PARTNERS[i]
        tc = lax.rem(c + oc, 2)
        tq, tb = pair_of(z, tc)
        px, pb = wrap(x + dx, NX), lax.rem(tb + db, 2)
        return px * NR + 2 * pb + tc, x * NR + 2 * tb + c, at_z(y, px, in_pair(tq, pb, tc), tc)

    def source(i):
        oc, db, dx = PARTNERS[i]
        px, pb, pc = wrap(x + dx, NX), lax.rem(b + db, 2), lax.rem(c + oc, 2)
        return px * NR + 2 * pb + pc, at_z(y, px, in_pair(q, pb, c), pc)

    loads = [
        pltpu.make_async_copy(x_hbm.at[:, pl.ds(k * WIDE, WIDE)], xin.at[k], load_sem.at[k])
        for k in range(CHUNKS)
    ]
    for copy in loads:
        copy.start()
    rows[:, 16:PAD, :] = jnp.zeros((GROUP, PAD - 16, D), BF16)

    barrier = pltpu.get_barrier_semaphore()

    def greet(device):
        pl.semaphore_signal(barrier, inc=1, device_id=device, device_id_type=MESH)

    def owner_z(sq):
        return in_pair(sq, zb, c)

    def home_z(sx):
        return 2 * sx + b

    for i in range(len(PARTNERS)):
        greet(source(i)[1])
    greet(up)
    greet(down)
    expected = len(PARTNERS) + 2
    for n in range(4):
        w_remote = jnp.logical_or(n != x, home_z(x) != z)
        r_remote = owner_z(n) != z
        expected = expected + jnp.logical_or(zi != x, r_remote).astype(jnp.int32)
        expected = expected + (home_z(n) != z).astype(jnp.int32)

        @pl.when(w_remote)
        def _():
            greet(at_z(y, n, home_z(x), c))

        @pl.when(r_remote)
        def _():
            greet(at_z(y, x, owner_z(n), c))

    wide[...] = jnp.zeros_like(wide)
    wide[:, 0:160] = wp_ref[...].astype(F32)
    wwin[...] = pltpu.roll(wide[...], 32 * x, 1).astype(BF16)
    for tc in range(2):
        meta_own[tc] = jnp.zeros((8, 128), F32)
        meta_own[tc, 0:1, 0:SLOTS] = tags_ref[...].astype(F32)
        meta_own[tc, 1:2, 0:SLOTS] = depths_ref[...].astype(F32)
        count = counts_ref[...]
        lane = lax.broadcasted_iota(jnp.int32, (1, SLOTS), 1)
        meta_own[tc, 2:3, 0:SLOTS] = jnp.where(lane < count, 1.0 / count.astype(F32), 0.0)
        meta_own[tc] = pltpu.roll(meta_own[tc], 32 * (2 * pair_of(z, tc)[1] + c), 1)
    pl.semaphore_wait(barrier, expected)

    def w_send(sq):
        device = at_z(y, zi, owner_z(sq), c)
        return (
            send(wwin, wxp.at[x], wp_s.at[sq], wp_r.at[x], device),
            send(wd_ref, wxd.at[x], wd_s.at[sq], wd_r.at[x], device),
        )

    def w_goes(sq):
        return jnp.logical_or(zi != x, owner_z(sq) != z)

    for sq in range(NQ):
        @pl.when(w_goes(sq))
        def _():
            for copy in w_send(sq):
                copy.start()

    @pl.when(jnp.logical_and(home_z(x) == z, zi == x))
    def _():
        wxp[x] = wwin[...]
        wxd[x] = wd_ref[...]

    def meta_send(i):
        _, slot, device = target(i)
        mine_for = meta_own.at[lax.rem(c + PARTNERS[i][0], 2)]
        return send(mine_for, meta_in.at[slot], meta_s.at[i], meta_r.at[slot], device)

    for i in range(len(PARTNERS)):
        meta_send(i).start()
    meta_in[me] = meta_own[c]

    ri = lax.broadcasted_iota(jnp.int32, (256, 256), 0)
    ci = lax.broadcasted_iota(jnp.int32, (256, 256), 1)
    turn = jnp.where(ci == lax.rem(ri, 16) * 16 + lax.div(ri, 16), 1.0, 0.0).astype(BF16)

    def act_send(k, i, j):
        layer, slot, device = target(i)
        lo, n = PARTS[j]
        return send(
            outbox.at[k, layer, pl.ds(lo, n)],
            rows.at[slot, pl.ds(lo, n), pl.ds(k * WIDE, WIDE)],
            act_s.at[k, i, j], act_r.at[k, slot, j], device,
        )

    def turn_and_send(k):
        loads[k].wait()

        @pl.loop(0, WIDE // 256)
        def _(n):
            cols = pl.ds(pl.multiple_of(n * 256, 256), 256)
            first = jnp.dot(turn, xin[k, 0:256, cols], preferred_element_type=F32)
            outbox[k, :, 0:16, cols] = first.astype(BF16).reshape(16, 16, 256)
            last = jnp.dot(turn[:, 0:192], xin[k, 256:448, cols], preferred_element_type=F32)
            outbox[k, :, 16:32, cols] = last.astype(BF16).reshape(16, 16, 256)

        for i in range(len(PARTNERS)):
            for j in range(2):
                act_send(k, i, j).start()
        rows[me, :, k * WIDE:(k + 1) * WIDE] = outbox[k, me]

    for k in range(CHUNKS):
        turn_and_send(k)

    for sx in range(NX):
        @pl.when(jnp.logical_or(sx != x, home_z(x) != z))
        def _():
            device = at_z(y, sx, home_z(x), c)
            send(wwin, wxp.at[sx], wp_s.at[0], wp_r.at[sx], device).wait_recv()
            send(wd_ref, wxd.at[sx], wd_s.at[0], wd_r.at[sx], device).wait_recv()
    for t in range(5):
        part = None
        for sx in (t - 1, t):
            if 0 <= sx < NX:
                lo = 128 * (t - sx)
                v = wxp[sx, :, lo:lo + 128].astype(F32)
                part = v if part is None else part + v
        wf[y, 0:TAGS, 128 * t:128 * (t + 1)] = part.astype(BF16)
    wf[y, TAGS:K] = wxd[...].reshape(OWN, RANK).astype(F32).T.astype(BF16)

    def ring(s, way):
        at = wrap(y - s, NY) if way > 0 else wrap(y + s, NY)
        ss, rs = (wr_s, wr_r) if way > 0 else (wl_s, wl_r)
        return send(wf.at[at], wf.at[at], ss.at[s], rs.at[s], up if way > 0 else down)

    for s in range(4):
        for way, steps in ((1, 4), (-1, 3)):
            if s < steps:
                if s > 0:
                    ring(s - 1, way).wait_recv()
                ring(s, way).start()
    ring(3, 1).wait_recv()
    ring(2, -1).wait_recv()

    acc[...] = jnp.zeros_like(acc)

    @pl.loop(0, CHUNKS)
    def _(k):
        for i in range(len(PARTNERS)):
            slot, device = source(i)
            for j, (lo, n) in enumerate(PARTS):
                send(
                    outbox.at[0, slot, pl.ds(lo, n)],
                    rows.at[slot, pl.ds(lo, n), pl.ds(pl.multiple_of(k * WIDE, WIDE), WIDE)],
                    act_s.at[k, i, j], act_r.at[k, slot, j], device,
                ).wait_recv()
        for h in range(2):
            cols = pl.ds(pl.multiple_of(k * WIDE + h * OWN, 128), OWN)
            acc[...] += lax.dot_general(
                wf[2 * k + h], rows[:, :, cols].reshape(GROUP * PAD, OWN),
                (((1,), (1,)), ((), ())), preferred_element_type=F32,
            )

    for i in range(len(PARTNERS)):
        slot, device = source(i)
        send(meta_own.at[0], meta_in.at[slot], meta_s.at[i], meta_r.at[slot], device).wait_recv()
    facts = jnp.concatenate(
        [sum(meta_in[NR * sx + sr] for sr in range(NR)) for sx in range(NX)], axis=1
    )
    tags, depths, scale = facts[0:1], facts[1:2], facts[2:3]
    logits, hidden = acc[0:TAGS], acc[TAGS:K]
    expo = jnp.exp(logits - jnp.max(logits, axis=0, keepdims=True))
    probs = expo / jnp.sum(expo, axis=0, keepdims=True)
    names = lax.broadcasted_iota(jnp.int32, (TAGS, GROUP * PAD), 0).astype(F32)
    onehot = jnp.where(names == tags, 1.0, 0.0)
    g_ref[0:TAGS] = ((probs - onehot) * scale).astype(BF16)
    predicted = jnp.sum(hidden * hidden, axis=0, keepdims=True)
    g_ref[TAGS:K] = (hidden * ((predicted - depths) * scale)).astype(BF16)

    def block(at, sub):
        lo, n = sub
        cols = pl.ds(pl.multiple_of(at * OWN, 128), OWN)
        return jnp.dot(
            g_ref[lo:lo + n], rows[:, :, cols].reshape(GROUP * PAD, OWN), preferred_element_type=F32
        )

    def hop(s, u, way):
        lo, n = SUBS[u]
        out, inn, ss, rs = (right_out, right_in, rr_s, rr_r) if way > 0 else (left_out, left_in, rl_s, rl_r)
        return send(
            out.at[s, pl.ds(lo, n)], inn.at[s, pl.ds(lo, n)], ss.at[s, u], rs.at[s, u],
            up if way > 0 else down,
        )

    for s in range(4):
        for u, (lo, n) in enumerate(SUBS):
            for way, steps in ((1, 4), (-1, 3)):
                if s >= steps:
                    continue
                out, inn = (right_out, right_in) if way > 0 else (left_out, left_in)
                at = wrap(y + 4 - s, NY) if way > 0 else wrap(y - 3 + s, NY)
                value = block(at, (lo, n))
                if s > 0:
                    hop(s - 1, u, way).wait_recv()
                    value = value + inn[s - 1, lo:lo + n].astype(F32)
                out[s, lo:lo + n] = value.astype(BF16)
                hop(s, u, way).start()
    def window(sx):
        return pl.ds(pl.multiple_of(128 * sx, 128), 256)

    def r2(u, dx):
        px, part = wrap(x + dx, NX), pl.ds(*SUBS[u])
        return send(
            mine.at[part, window(px)], r2_in.at[x, part], r2_s.at[u, dx], r2_r.at[u, x], at_z(y, px, z, c)
        )

    def r3(u, sx):
        part = pl.ds(*SUBS[u])
        return send(
            r2_in.at[sx, part], r3_in.at[q, part], r3_s.at[u, sx], r3_r.at[u, q], at_z(y, x, home_z(sx), c)
        )

    def forward(u):
        lo, n = SUBS[u]
        for dx in (0, 1, 3, 2):
            sx = wrap(x + dx, NX)
            if dx:
                send(
                    mine.at[pl.ds(lo, n), pl.ds(0, 256)], r2_in.at[sx, pl.ds(lo, n)],
                    r2_s.at[u, dx], r2_r.at[u, sx], at_z(y, sx, z, c),
                ).wait_recv()

            @pl.when(home_z(sx) != z)
            def _():
                r3(u, sx).start()

            @pl.when(home_z(sx) == z)
            def _():
                r3_in[q, lo:lo + n] = r2_in[sx, lo:lo + n]

    for u, (lo, n) in enumerate(SUBS):
        value = block(y, (lo, n))
        hop(2, u, -1).wait_recv()
        value = value + left_in[2, lo:lo + n].astype(F32)
        hop(3, u, 1).wait_recv()
        mine[lo:lo + n] = (value + right_in[3, lo:lo + n].astype(F32)).astype(BF16)
        for dx in (1, 3, 2):
            r2(u, dx).start()
        r2_in[x, lo:lo + n] = mine[lo:lo + n, window(x)]
        if u:
            forward(u - 1)
    forward(len(SUBS) - 1)
    for u, (lo, n) in enumerate(SUBS):
        total = jnp.zeros((n, 256), F32)
        for sq in range(NQ):
            @pl.when(owner_z(sq) != z)
            def _():
                send(
                    r2_in.at[0, pl.ds(lo, n)], r3_in.at[sq, pl.ds(lo, n)],
                    r3_s.at[u, 0], r3_r.at[u, sq], at_z(y, x, owner_z(sq), c),
                ).wait_recv()
            total = total + r3_in[sq, lo:lo + n].astype(F32)
        total = pltpu.roll(total, lax.rem(256 - 32 * x, 256), 1)
        if u == 0:
            pos_out[...] = total[:, 0:160]
        else:
            acc[lo:lo + n, 0:256] = total
    dep_out[...] = acc[TAGS:K, 0:256].T[0:160]

    for sq in range(NQ):
        @pl.when(w_goes(sq))
        def _():
            for copy in w_send(sq):
                copy.wait_send()
    for i in range(len(PARTNERS)):
        meta_send(i).wait_send()
        for k in range(CHUNKS):
            for j in range(2):
                act_send(k, i, j).wait_send()
    for s in range(4):
        for way, steps in ((1, 4), (-1, 3)):
            if s < steps:
                ring(s, way).wait_send()
                for u in range(len(SUBS)):
                    hop(s, u, way).wait_send()
    for u in range(len(SUBS)):
        for dx in (1, 3, 2):
            r2(u, dx).wait_send()
        for sx in range(NX):
            @pl.when(home_z(sx) != z)
            def _():
                r3(u, sx).wait_send()


def local(activations, pos_weight, depth_weight, tags, depths, counts):
    acts = jnp.transpose(activations, (1, 0, 2)).reshape(SLOTS * 16, D)
    dma, vm = pltpu.SemaphoreType.DMA, pltpu.VMEM
    in_vmem = pl.BlockSpec(memory_space=vm)
    pos, dep = pl.pallas_call(
        kernel,
        out_shape=(jax.ShapeDtypeStruct((TAGS, 160), F32), jax.ShapeDtypeStruct((160, RANK), F32)),
        in_specs=[pl.BlockSpec(memory_space=pl.ANY)] + [in_vmem] * 5,
        out_specs=(in_vmem, in_vmem),
        scratch_shapes=[
            vm((CHUNKS, SLOTS * 16, WIDE), BF16), vm((CHUNKS, 16, PAD, WIDE), BF16), vm((GROUP, PAD, D), BF16),
            vm((TAGS, 256), F32), vm((TAGS, 256), BF16), vm((NX, TAGS, 256), BF16), vm((NX, 160, RANK), BF16),
            vm((NY, K, OWN), BF16),
            vm((2, 8, 128), F32), vm((GROUP, 8, 128), F32), vm((K, GROUP * PAD), F32), vm((K, GROUP * PAD), BF16),
            vm((4, K, OWN), BF16), vm((4, K, OWN), BF16), vm((3, K, OWN), BF16), vm((3, K, OWN), BF16),
            vm((K, OWN), BF16), vm((NX, K, 256), BF16), vm((NQ, K, 256), BF16),
            dma((CHUNKS,)), dma((CHUNKS, 15, 2)), dma((CHUNKS, GROUP, 2)),
            dma((NQ,)), dma((NX,)), dma((NQ,)), dma((NX,)),
            dma((4,)), dma((4,)), dma((3,)), dma((3,)), dma((15,)), dma((GROUP,)),
            dma((4, 4)), dma((4, 4)), dma((3, 4)), dma((3, 4)), dma((4, 4)), dma((4, NX)), dma((4, NX)), dma((4, NQ)),
        ],
        compiler_params=pltpu.CompilerParams(
            collective_id=0, has_side_effects=True, vmem_limit_bytes=61 * 1024 * 1024
        ),
    )(
        acts, pos_weight[0], depth_weight[0].T,
        tags.reshape(1, SLOTS), depths.reshape(1, SLOTS), counts.reshape(1, 1),
    )
    return pos[None], dep.T[None]


def solution(mesh):
    in_specs = (
        P(None, ("tok", "layer"), None),
        P("layer", None, "tok"),
        P("layer", None, "tok"),
        P(("tok", "layer")),
        P(("tok", "layer")),
        P(("tok", "layer")),
    )
    out_specs = (P("layer", None, "tok"), P("layer", None, "tok"))
    return jax.shard_map(local, mesh=mesh, in_specs=in_specs, out_specs=out_specs, check_vma=False)
```

```python
import jax
import jax.numpy as jnp
from jax import lax
from jax.experimental import pallas as pl
from jax.experimental.pallas import tpu as pltpu
from jax.sharding import PartitionSpec as P

MESH = pl.DeviceIdType.MESH
F32, BF16 = jnp.float32, jnp.bfloat16

D, TAGS, RANK, SLOTS = 5120, 48, 128, 28
K = TAGS + RANK
PAD = 32
NX, NY, NQ, NR = 4, 8, 4, 4
GROUP = NX * NR
CHUNKS, WIDE = 4, D // 4
AHEAD = 2
OWN = D // NY
SUBS = ((0, 48), (48, 48), (96, 48), (144, 32))
PARTS = ((0, 24), (24, 4))
PARTNERS = tuple(
    (oc, db, dx) for oc in (0, 1) for db in (0, 1) for dx in (1, 3, 2, 0) if (oc, db, dx) != (0, 0, 0)
)


def wrap(v, n):
    return lax.rem(v + n, n)


def at_z(y, x, z, c):
    return {"tok": y * NX + x, "layer": 2 * z + c}


def pair_of(z, c):
    shifted = wrap(z - c, 8)
    return lax.div(shifted, 2), lax.rem(shifted, 2)


def in_pair(q, b, c):
    return lax.rem(2 * q + b + c, 8)


def send(src, dst, ssem, rsem, device):
    return pltpu.make_async_remote_copy(
        src_ref=src, dst_ref=dst, send_sem=ssem, recv_sem=rsem, device_id=device, device_id_type=MESH
    )


def kernel(
    x_hbm, wp_ref, wd_ref, tags_ref, depths_ref, counts_ref, pos_out, dep_out,
    xin, outbox, rows, wide, wwin, wxp, wxd, wf, meta_own, meta_in, acc, g_ref,
    right_out, right_in, left_out, left_in, mine, r2_in, r3_in,
    load_sem, act_s, act_r, wp_s, wp_r, wd_s, wd_r, wr_s, wr_r, wl_s, wl_r, meta_s, meta_r,
    rr_s, rr_r, rl_s, rl_r, r2_s, r2_r, r3_s, r3_r,
):
    tok, lay = lax.axis_index("tok"), lax.axis_index("layer")
    y, x, z, c = lax.div(tok, NX), lax.rem(tok, NX), lax.div(lay, 2), lax.rem(lay, 2)
    q, b = pair_of(z, c)
    me = x * NR + 2 * b + c
    zi, zb = lax.div(z, 2), lax.rem(z, 2)
    up, down = at_z(wrap(y + 1, NY), x, z, c), at_z(wrap(y - 1, NY), x, z, c)

    def target(i):
        oc, db, dx = PARTNERS[i]
        tc = lax.rem(c + oc, 2)
        tq, tb = pair_of(z, tc)
        px, pb = wrap(x + dx, NX), lax.rem(tb + db, 2)
        return px * NR + 2 * pb + tc, x * NR + 2 * tb + c, at_z(y, px, in_pair(tq, pb, tc), tc)

    def source(i):
        oc, db, dx = PARTNERS[i]
        px, pb, pc = wrap(x + dx, NX), lax.rem(b + db, 2), lax.rem(c + oc, 2)
        return px * NR + 2 * pb + pc, at_z(y, px, in_pair(q, pb, c), pc)

    loads = [
        pltpu.make_async_copy(x_hbm.at[:, pl.ds(k * WIDE, WIDE)], xin.at[k], load_sem.at[k])
        for k in range(CHUNKS)
    ]
    for copy in loads:
        copy.start()
    rows[:, 16:PAD, :] = jnp.zeros((GROUP, PAD - 16, D), BF16)

    barrier = pltpu.get_barrier_semaphore()

    def greet(device):
        pl.semaphore_signal(barrier, inc=1, device_id=device, device_id_type=MESH)

    def owner_z(sq):
        return in_pair(sq, zb, c)

    def home_z(sx):
        return 2 * sx + b

    for i in range(len(PARTNERS)):
        greet(source(i)[1])
    greet(up)
    greet(down)
    expected = len(PARTNERS) + 2
    for n in range(4):
        w_remote = jnp.logical_or(n != x, home_z(x) != z)
        r_remote = owner_z(n) != z
        expected = expected + jnp.logical_or(zi != x, r_remote).astype(jnp.int32)
        expected = expected + (home_z(n) != z).astype(jnp.int32)

        @pl.when(w_remote)
        def _():
            greet(at_z(y, n, home_z(x), c))

        @pl.when(r_remote)
        def _():
            greet(at_z(y, x, owner_z(n), c))

    wide[...] = jnp.zeros_like(wide)
    wide[:, 0:160] = wp_ref[...].astype(F32)
    wwin[...] = pltpu.roll(wide[...], 32 * x, 1).astype(BF16)
    for tc in range(2):
        meta_own[tc] = jnp.zeros((8, 128), F32)
        meta_own[tc, 0:1, 0:SLOTS] = tags_ref[...].astype(F32)
        meta_own[tc, 1:2, 0:SLOTS] = depths_ref[...].astype(F32)
        count = counts_ref[...]
        lane = lax.broadcasted_iota(jnp.int32, (1, SLOTS), 1)
        meta_own[tc, 2:3, 0:SLOTS] = jnp.where(lane < count, 1.0 / count.astype(F32), 0.0)
        meta_own[tc] = pltpu.roll(meta_own[tc], 32 * (2 * pair_of(z, tc)[1] + c), 1)
    ri = lax.broadcasted_iota(jnp.int32, (256, 256), 0)
    ci = lax.broadcasted_iota(jnp.int32, (256, 256), 1)
    turn = jnp.where(ci == lax.rem(ri, 16) * 16 + lax.div(ri, 16), 1.0, 0.0).astype(BF16)

    def relay(k):
        loads[k].wait()

        @pl.loop(0, WIDE // 256)
        def _(n):
            cols = pl.ds(pl.multiple_of(n * 256, 256), 256)
            head = jnp.dot(turn, xin[k, 0:256, cols], preferred_element_type=F32)
            outbox[k, :, 0:16, cols] = head.astype(BF16).reshape(16, 16, 256)
            last = jnp.dot(turn[:, 0:192], xin[k, 256:448, cols], preferred_element_type=F32)
            outbox[k, :, 16:32, cols] = last.astype(BF16).reshape(16, 16, 256)

    for k in range(AHEAD):
        relay(k)
    pl.semaphore_wait(barrier, expected)

    def w_send(sq):
        device = at_z(y, zi, owner_z(sq), c)
        return (
            send(wwin, wxp.at[x], wp_s.at[sq], wp_r.at[x], device),
            send(wd_ref, wxd.at[x], wd_s.at[sq], wd_r.at[x], device),
        )

    def w_goes(sq):
        return jnp.logical_or(zi != x, owner_z(sq) != z)

    for sq in range(NQ):
        @pl.when(w_goes(sq))
        def _():
            for copy in w_send(sq):
                copy.start()

    @pl.when(jnp.logical_and(home_z(x) == z, zi == x))
    def _():
        wxp[x] = wwin[...]
        wxd[x] = wd_ref[...]

    def meta_send(i):
        _, slot, device = target(i)
        mine_for = meta_own.at[lax.rem(c + PARTNERS[i][0], 2)]
        return send(mine_for, meta_in.at[slot], meta_s.at[i], meta_r.at[slot], device)

    for i in range(len(PARTNERS)):
        meta_send(i).start()
    meta_in[me] = meta_own[c]

    def act_send(k, i, j):
        layer, slot, device = target(i)
        lo, n = PARTS[j]
        return send(
            outbox.at[k, layer, pl.ds(lo, n)],
            rows.at[slot, pl.ds(lo, n), pl.ds(k * WIDE, WIDE)],
            act_s.at[k, i, j], act_r.at[k, slot, j], device,
        )

    for k in range(CHUNKS):
        if k >= AHEAD:
            relay(k)
        for i in range(len(PARTNERS)):
            for j in range(2):
                act_send(k, i, j).start()
        rows[me, :, k * WIDE:(k + 1) * WIDE] = outbox[k, me]

    for sx in range(NX):
        @pl.when(jnp.logical_or(sx != x, home_z(x) != z))
        def _():
            device = at_z(y, sx, home_z(x), c)
            send(wwin, wxp.at[sx], wp_s.at[0], wp_r.at[sx], device).wait_recv()
            send(wd_ref, wxd.at[sx], wd_s.at[0], wd_r.at[sx], device).wait_recv()
    for t in range(5):
        part = None
        for sx in (t - 1, t):
            if 0 <= sx < NX:
                lo = 128 * (t - sx)
                v = wxp[sx, :, lo:lo + 128].astype(F32)
                part = v if part is None else part + v
        wf[y, 0:TAGS, 128 * t:128 * (t + 1)] = part.astype(BF16)
    wf[y, TAGS:K] = wxd[...].reshape(OWN, RANK).astype(F32).T.astype(BF16)

    def ring(s, way):
        at = wrap(y - s, NY) if way > 0 else wrap(y + s, NY)
        ss, rs = (wr_s, wr_r) if way > 0 else (wl_s, wl_r)
        return send(wf.at[at], wf.at[at], ss.at[s], rs.at[s], up if way > 0 else down)

    for s in range(4):
        for way, steps in ((1, 4), (-1, 3)):
            if s < steps:
                if s > 0:
                    ring(s - 1, way).wait_recv()
                ring(s, way).start()
    ring(3, 1).wait_recv()
    ring(2, -1).wait_recv()

    acc[...] = jnp.zeros_like(acc)

    @pl.loop(0, CHUNKS)
    def _(k):
        for i in range(len(PARTNERS)):
            slot, device = source(i)
            for j, (lo, n) in enumerate(PARTS):
                send(
                    outbox.at[0, slot, pl.ds(lo, n)],
                    rows.at[slot, pl.ds(lo, n), pl.ds(pl.multiple_of(k * WIDE, WIDE), WIDE)],
                    act_s.at[k, i, j], act_r.at[k, slot, j], device,
                ).wait_recv()
        for h in range(2):
            cols = pl.ds(pl.multiple_of(k * WIDE + h * OWN, 128), OWN)
            acc[...] += lax.dot_general(
                wf[2 * k + h], rows[:, :, cols].reshape(GROUP * PAD, OWN),
                (((1,), (1,)), ((), ())), preferred_element_type=F32,
            )

    for i in range(len(PARTNERS)):
        slot, device = source(i)
        send(meta_own.at[0], meta_in.at[slot], meta_s.at[i], meta_r.at[slot], device).wait_recv()
    facts = jnp.concatenate(
        [sum(meta_in[NR * sx + sr] for sr in range(NR)) for sx in range(NX)], axis=1
    )
    tags, depths, scale = facts[0:1], facts[1:2], facts[2:3]
    logits, hidden = acc[0:TAGS], acc[TAGS:K]
    expo = jnp.exp(logits - jnp.max(logits, axis=0, keepdims=True))
    probs = expo / jnp.sum(expo, axis=0, keepdims=True)
    names = lax.broadcasted_iota(jnp.int32, (TAGS, GROUP * PAD), 0).astype(F32)
    onehot = jnp.where(names == tags, 1.0, 0.0)
    g_ref[0:TAGS] = ((probs - onehot) * scale).astype(BF16)
    predicted = jnp.sum(hidden * hidden, axis=0, keepdims=True)
    g_ref[TAGS:K] = (hidden * ((predicted - depths) * scale)).astype(BF16)

    def block(at, sub):
        lo, n = sub
        cols = pl.ds(pl.multiple_of(at * OWN, 128), OWN)
        return jnp.dot(
            g_ref[lo:lo + n], rows[:, :, cols].reshape(GROUP * PAD, OWN), preferred_element_type=F32
        )

    def hop(s, u, way):
        lo, n = SUBS[u]
        out, inn, ss, rs = (right_out, right_in, rr_s, rr_r) if way > 0 else (left_out, left_in, rl_s, rl_r)
        return send(
            out.at[s, pl.ds(lo, n)], inn.at[s, pl.ds(lo, n)], ss.at[s, u], rs.at[s, u],
            up if way > 0 else down,
        )

    def first(u, way):
        return 0 if (u < 2) == (way > 0) else 1

    for s in range(4):
        for u, (lo, n) in enumerate(SUBS):
            for way in (1, -1):
                if s < first(u, way):
                    continue
                out, inn = (right_out, right_in) if way > 0 else (left_out, left_in)
                value = block(wrap(y + way * (4 - s), NY), (lo, n))
                if s > first(u, way):
                    hop(s - 1, u, way).wait_recv()
                    value = value + inn[s - 1, lo:lo + n].astype(F32)
                out[s, lo:lo + n] = value.astype(BF16)
                hop(s, u, way).start()
    def window(sx):
        return pl.ds(pl.multiple_of(128 * sx, 128), 256)

    def r2(u, dx):
        px, part = wrap(x + dx, NX), pl.ds(*SUBS[u])
        return send(
            mine.at[part, window(px)], r2_in.at[x, part], r2_s.at[u, dx], r2_r.at[u, x], at_z(y, px, z, c)
        )

    def r3(u, sx):
        part = pl.ds(*SUBS[u])
        return send(
            r2_in.at[sx, part], r3_in.at[q, part], r3_s.at[u, sx], r3_r.at[u, q], at_z(y, x, home_z(sx), c)
        )

    def forward(u):
        lo, n = SUBS[u]
        for dx in (0, 1, 3, 2):
            sx = wrap(x + dx, NX)
            if dx:
                send(
                    mine.at[pl.ds(lo, n), pl.ds(0, 256)], r2_in.at[sx, pl.ds(lo, n)],
                    r2_s.at[u, dx], r2_r.at[u, sx], at_z(y, sx, z, c),
                ).wait_recv()

            @pl.when(home_z(sx) != z)
            def _():
                r3(u, sx).start()

            @pl.when(home_z(sx) == z)
            def _():
                r3_in[q, lo:lo + n] = r2_in[sx, lo:lo + n]

    for u, (lo, n) in enumerate(SUBS):
        value = block(y, (lo, n))
        hop(3, u, -1).wait_recv()
        value = value + left_in[3, lo:lo + n].astype(F32)
        hop(3, u, 1).wait_recv()
        mine[lo:lo + n] = (value + right_in[3, lo:lo + n].astype(F32)).astype(BF16)
        for dx in (1, 3, 2):
            r2(u, dx).start()
        r2_in[x, lo:lo + n] = mine[lo:lo + n, window(x)]
        if u:
            forward(u - 1)
    forward(len(SUBS) - 1)
    for u, (lo, n) in enumerate(SUBS):
        total = jnp.zeros((n, 256), F32)
        for sq in range(NQ):
            @pl.when(owner_z(sq) != z)
            def _():
                send(
                    r2_in.at[0, pl.ds(lo, n)], r3_in.at[sq, pl.ds(lo, n)],
                    r3_s.at[u, 0], r3_r.at[u, sq], at_z(y, x, owner_z(sq), c),
                ).wait_recv()
            total = total + r3_in[sq, lo:lo + n].astype(F32)
        total = pltpu.roll(total, lax.rem(256 - 32 * x, 256), 1)
        if u == 0:
            pos_out[...] = total[:, 0:160]
        else:
            acc[lo:lo + n, 0:256] = total
    dep_out[...] = acc[TAGS:K, 0:256].T[0:160]

    for sq in range(NQ):
        @pl.when(w_goes(sq))
        def _():
            for copy in w_send(sq):
                copy.wait_send()
    for i in range(len(PARTNERS)):
        meta_send(i).wait_send()
        for k in range(CHUNKS):
            for j in range(2):
                act_send(k, i, j).wait_send()
    for s in range(4):
        for way, steps in ((1, 4), (-1, 3)):
            if s < steps:
                ring(s, way).wait_send()
            for u in range(len(SUBS)):
                if s >= first(u, way):
                    hop(s, u, way).wait_send()
    for u in range(len(SUBS)):
        for dx in (1, 3, 2):
            r2(u, dx).wait_send()
        for sx in range(NX):
            @pl.when(home_z(sx) != z)
            def _():
                r3(u, sx).wait_send()


def local(activations, pos_weight, depth_weight, tags, depths, counts):
    acts = jnp.transpose(activations, (1, 0, 2)).reshape(SLOTS * 16, D)
    dma, vm = pltpu.SemaphoreType.DMA, pltpu.VMEM
    in_vmem = pl.BlockSpec(memory_space=vm)
    pos, dep = pl.pallas_call(
        kernel,
        out_shape=(jax.ShapeDtypeStruct((TAGS, 160), F32), jax.ShapeDtypeStruct((160, RANK), F32)),
        in_specs=[pl.BlockSpec(memory_space=pl.ANY)] + [in_vmem] * 5,
        out_specs=(in_vmem, in_vmem),
        scratch_shapes=[
            vm((CHUNKS, SLOTS * 16, WIDE), BF16), vm((CHUNKS, 16, PAD, WIDE), BF16), vm((GROUP, PAD, D), BF16),
            vm((TAGS, 256), F32), vm((TAGS, 256), BF16), vm((NX, TAGS, 256), BF16), vm((NX, 160, RANK), BF16),
            vm((NY, K, OWN), BF16),
            vm((2, 8, 128), F32), vm((GROUP, 8, 128), F32), vm((K, GROUP * PAD), F32), vm((K, GROUP * PAD), BF16),
            vm((4, K, OWN), BF16), vm((4, K, OWN), BF16), vm((4, K, OWN), BF16), vm((4, K, OWN), BF16),
            vm((K, OWN), BF16), vm((NX, K, 256), BF16), vm((NQ, K, 256), BF16),
            dma((CHUNKS,)), dma((CHUNKS, 15, 2)), dma((CHUNKS, GROUP, 2)),
            dma((NQ,)), dma((NX,)), dma((NQ,)), dma((NX,)),
            dma((4,)), dma((4,)), dma((3,)), dma((3,)), dma((15,)), dma((GROUP,)),
            dma((4, 4)), dma((4, 4)), dma((4, 4)), dma((4, 4)), dma((4, 4)), dma((4, NX)), dma((4, NX)), dma((4, NQ)),
        ],
        compiler_params=pltpu.CompilerParams(
            collective_id=0, has_side_effects=True, vmem_limit_bytes=61 * 1024 * 1024
        ),
    )(
        acts, pos_weight[0], depth_weight[0].T,
        tags.reshape(1, SLOTS), depths.reshape(1, SLOTS), counts.reshape(1, 1),
    )
    return pos[None], dep.T[None]


def solution(mesh):
    in_specs = (
        P(None, ("tok", "layer"), None),
        P("layer", None, "tok"),
        P("layer", None, "tok"),
        P(("tok", "layer")),
        P(("tok", "layer")),
        P(("tok", "layer")),
    )
    out_specs = (P("layer", None, "tok"), P("layer", None, "tok"))
    return jax.shard_map(local, mesh=mesh, in_specs=in_specs, out_specs=out_specs, check_vma=False)
```

```python
import jax
import jax.numpy as jnp
from jax import lax
from jax.experimental import pallas as pl
from jax.experimental.pallas import tpu as pltpu
from jax.sharding import PartitionSpec as P

MESH = pl.DeviceIdType.MESH
F32, BF16 = jnp.float32, jnp.bfloat16

D, TAGS, RANK, SLOTS = 5120, 48, 128, 28
K = TAGS + RANK
PAD = 32
NX, NY, NQ, NR = 4, 8, 4, 4
GROUP = NX * NR
CHUNKS, WIDE = 4, D // 4
AHEAD = 2
OWN = D // NY
SUBS = ((0, 48), (48, 48), (96, 48), (144, 32))
PARTS = ((0, 24), (24, 4))
PARTNERS = tuple(
    (oc, db, dx) for db in (1, 0) for oc in (0, 1) for dx in (2, 1, 3, 0) if (oc, db, dx) != (0, 0, 0)
)


def wrap(v, n):
    return lax.rem(v + n, n)


def at_z(y, x, z, c):
    return {"tok": y * NX + x, "layer": 2 * z + c}


def pair_of(z, c):
    shifted = wrap(z - c, 8)
    return lax.div(shifted, 2), lax.rem(shifted, 2)


def in_pair(q, b, c):
    return lax.rem(2 * q + b + c, 8)


def send(src, dst, ssem, rsem, device):
    return pltpu.make_async_remote_copy(
        src_ref=src, dst_ref=dst, send_sem=ssem, recv_sem=rsem, device_id=device, device_id_type=MESH
    )


def kernel(
    x_hbm, wp_ref, wd_ref, tags_ref, depths_ref, counts_ref, pos_out, dep_out,
    xin, outbox, rows, wide, wwin, wxp, wxd, wf, meta_own, meta_in, acc, g_ref,
    right_out, right_in, left_out, left_in, mine, r2_in, r3_in,
    load_sem, act_s, act_r, wp_s, wp_r, wd_s, wd_r, wr_s, wr_r, wl_s, wl_r, meta_s, meta_r,
    rr_s, rr_r, rl_s, rl_r, r2_s, r2_r, r3_s, r3_r,
):
    tok, lay = lax.axis_index("tok"), lax.axis_index("layer")
    y, x, z, c = lax.div(tok, NX), lax.rem(tok, NX), lax.div(lay, 2), lax.rem(lay, 2)
    q, b = pair_of(z, c)
    me = x * NR + 2 * b + c
    zi, zb = lax.div(z, 2), lax.rem(z, 2)
    up, down = at_z(wrap(y + 1, NY), x, z, c), at_z(wrap(y - 1, NY), x, z, c)

    def target(i):
        oc, db, dx = PARTNERS[i]
        tc = lax.rem(c + oc, 2)
        tq, tb = pair_of(z, tc)
        px, pb = wrap(x + dx, NX), lax.rem(tb + db, 2)
        return px * NR + 2 * pb + tc, x * NR + 2 * tb + c, at_z(y, px, in_pair(tq, pb, tc), tc)

    def source(i):
        oc, db, dx = PARTNERS[i]
        px, pb, pc = wrap(x + dx, NX), lax.rem(b + db, 2), lax.rem(c + oc, 2)
        return px * NR + 2 * pb + pc, at_z(y, px, in_pair(q, pb, c), pc)

    loads = [
        pltpu.make_async_copy(x_hbm.at[:, pl.ds(k * WIDE, WIDE)], xin.at[k], load_sem.at[k])
        for k in range(CHUNKS)
    ]
    for copy in loads:
        copy.start()
    rows[:, 16:PAD, :] = jnp.zeros((GROUP, PAD - 16, D), BF16)

    barrier = pltpu.get_barrier_semaphore()

    def greet(device):
        pl.semaphore_signal(barrier, inc=1, device_id=device, device_id_type=MESH)

    def owner_z(sq):
        return in_pair(sq, zb, c)

    def home_z(sx):
        return 2 * sx + b

    for i in range(len(PARTNERS)):
        greet(source(i)[1])
    greet(up)
    greet(down)
    expected = len(PARTNERS) + 2
    for n in range(4):
        w_remote = jnp.logical_or(n != x, home_z(x) != z)
        r_remote = owner_z(n) != z
        expected = expected + jnp.logical_or(zi != x, r_remote).astype(jnp.int32)
        expected = expected + (home_z(n) != z).astype(jnp.int32)

        @pl.when(w_remote)
        def _():
            greet(at_z(y, n, home_z(x), c))

        @pl.when(r_remote)
        def _():
            greet(at_z(y, x, owner_z(n), c))

    wide[...] = jnp.zeros_like(wide)
    wide[:, 0:160] = wp_ref[...].astype(F32)
    wwin[...] = pltpu.roll(wide[...], 32 * x, 1).astype(BF16)
    for tc in range(2):
        meta_own[tc] = jnp.zeros((8, 128), F32)
        meta_own[tc, 0:1, 0:SLOTS] = tags_ref[...].astype(F32)
        meta_own[tc, 1:2, 0:SLOTS] = depths_ref[...].astype(F32)
        count = counts_ref[...]
        lane = lax.broadcasted_iota(jnp.int32, (1, SLOTS), 1)
        meta_own[tc, 2:3, 0:SLOTS] = jnp.where(lane < count, 1.0 / count.astype(F32), 0.0)
        meta_own[tc] = pltpu.roll(meta_own[tc], 32 * (2 * pair_of(z, tc)[1] + c), 1)
    ri = lax.broadcasted_iota(jnp.int32, (256, 256), 0)
    ci = lax.broadcasted_iota(jnp.int32, (256, 256), 1)
    turn = jnp.where(ci == lax.rem(ri, 16) * 16 + lax.div(ri, 16), 1.0, 0.0).astype(BF16)

    def relay(k):
        loads[k].wait()

        @pl.loop(0, WIDE // 256)
        def _(n):
            cols = pl.ds(pl.multiple_of(n * 256, 256), 256)
            head = jnp.dot(turn, xin[k, 0:256, cols], preferred_element_type=F32)
            outbox[k, :, 0:16, cols] = head.astype(BF16).reshape(16, 16, 256)
            last = jnp.dot(turn[:, 0:192], xin[k, 256:448, cols], preferred_element_type=F32)
            outbox[k, :, 16:32, cols] = last.astype(BF16).reshape(16, 16, 256)

    for k in range(AHEAD):
        relay(k)
    pl.semaphore_wait(barrier, expected)

    def w_send(sq):
        device = at_z(y, zi, owner_z(sq), c)
        return (
            send(wwin, wxp.at[x], wp_s.at[sq], wp_r.at[x], device),
            send(wd_ref, wxd.at[x], wd_s.at[sq], wd_r.at[x], device),
        )

    def w_goes(sq):
        return jnp.logical_or(zi != x, owner_z(sq) != z)

    for sq in range(NQ):
        @pl.when(w_goes(sq))
        def _():
            for copy in w_send(sq):
                copy.start()

    @pl.when(jnp.logical_and(home_z(x) == z, zi == x))
    def _():
        wxp[x] = wwin[...]
        wxd[x] = wd_ref[...]

    def meta_send(i):
        _, slot, device = target(i)
        mine_for = meta_own.at[lax.rem(c + PARTNERS[i][0], 2)]
        return send(mine_for, meta_in.at[slot], meta_s.at[i], meta_r.at[slot], device)

    for i in range(len(PARTNERS)):
        meta_send(i).start()
    meta_in[me] = meta_own[c]

    def act_send(k, i, j):
        layer, slot, device = target(i)
        lo, n = PARTS[j]
        return send(
            outbox.at[k, layer, pl.ds(lo, n)],
            rows.at[slot, pl.ds(lo, n), pl.ds(k * WIDE, WIDE)],
            act_s.at[k, i, j], act_r.at[k, slot, j], device,
        )

    for k in range(CHUNKS):
        if k >= AHEAD:
            relay(k)
        for i in range(len(PARTNERS)):
            for j in range(2):
                act_send(k, i, j).start()
        rows[me, :, k * WIDE:(k + 1) * WIDE] = outbox[k, me]

    for sx in range(NX):
        @pl.when(jnp.logical_or(sx != x, home_z(x) != z))
        def _():
            device = at_z(y, sx, home_z(x), c)
            send(wwin, wxp.at[sx], wp_s.at[0], wp_r.at[sx], device).wait_recv()
            send(wd_ref, wxd.at[sx], wd_s.at[0], wd_r.at[sx], device).wait_recv()
    for t in range(5):
        part = None
        for sx in (t - 1, t):
            if 0 <= sx < NX:
                lo = 128 * (t - sx)
                v = wxp[sx, :, lo:lo + 128].astype(F32)
                part = v if part is None else part + v
        wf[y, 0:TAGS, 128 * t:128 * (t + 1)] = part.astype(BF16)
    wf[y, TAGS:K] = wxd[...].reshape(OWN, RANK).astype(F32).T.astype(BF16)

    def ring(s, way):
        at = wrap(y - s, NY) if way > 0 else wrap(y + s, NY)
        ss, rs = (wr_s, wr_r) if way > 0 else (wl_s, wl_r)
        return send(wf.at[at], wf.at[at], ss.at[s], rs.at[s], up if way > 0 else down)

    for s in range(4):
        for way, steps in ((1, 4), (-1, 3)):
            if s < steps:
                if s > 0:
                    ring(s - 1, way).wait_recv()
                ring(s, way).start()
    ring(3, 1).wait_recv()
    ring(2, -1).wait_recv()

    acc[...] = jnp.zeros_like(acc)

    @pl.loop(0, CHUNKS)
    def _(k):
        for i in range(len(PARTNERS)):
            slot, device = source(i)
            for j, (lo, n) in enumerate(PARTS):
                send(
                    outbox.at[0, slot, pl.ds(lo, n)],
                    rows.at[slot, pl.ds(lo, n), pl.ds(pl.multiple_of(k * WIDE, WIDE), WIDE)],
                    act_s.at[k, i, j], act_r.at[k, slot, j], device,
                ).wait_recv()
        for h in range(2):
            cols = pl.ds(pl.multiple_of(k * WIDE + h * OWN, 128), OWN)
            acc[...] += lax.dot_general(
                wf[2 * k + h], rows[:, :, cols].reshape(GROUP * PAD, OWN),
                (((1,), (1,)), ((), ())), preferred_element_type=F32,
            )

    for i in range(len(PARTNERS)):
        slot, device = source(i)
        send(meta_own.at[0], meta_in.at[slot], meta_s.at[i], meta_r.at[slot], device).wait_recv()
    facts = jnp.concatenate(
        [sum(meta_in[NR * sx + sr] for sr in range(NR)) for sx in range(NX)], axis=1
    )
    tags, depths, scale = facts[0:1], facts[1:2], facts[2:3]
    logits, hidden = acc[0:TAGS], acc[TAGS:K]
    expo = jnp.exp(logits - jnp.max(logits, axis=0, keepdims=True))
    probs = expo / jnp.sum(expo, axis=0, keepdims=True)
    names = lax.broadcasted_iota(jnp.int32, (TAGS, GROUP * PAD), 0).astype(F32)
    onehot = jnp.where(names == tags, 1.0, 0.0)
    g_ref[0:TAGS] = ((probs - onehot) * scale).astype(BF16)
    predicted = jnp.sum(hidden * hidden, axis=0, keepdims=True)
    g_ref[TAGS:K] = (hidden * ((predicted - depths) * scale)).astype(BF16)

    def block(at, sub):
        lo, n = sub
        cols = pl.ds(pl.multiple_of(at * OWN, 128), OWN)
        return jnp.dot(
            g_ref[lo:lo + n], rows[:, :, cols].reshape(GROUP * PAD, OWN), preferred_element_type=F32
        )

    def hop(s, u, way):
        lo, n = SUBS[u]
        out, inn, ss, rs = (right_out, right_in, rr_s, rr_r) if way > 0 else (left_out, left_in, rl_s, rl_r)
        return send(
            out.at[s, pl.ds(lo, n)], inn.at[s, pl.ds(lo, n)], ss.at[s, u], rs.at[s, u],
            up if way > 0 else down,
        )

    def first(u, way):
        return 0 if (u < 2) == (way > 0) else 1

    for s in range(4):
        for u, (lo, n) in enumerate(SUBS):
            for way in (1, -1):
                if s < first(u, way):
                    continue
                out, inn = (right_out, right_in) if way > 0 else (left_out, left_in)
                value = block(wrap(y + way * (4 - s), NY), (lo, n))
                if s > first(u, way):
                    hop(s - 1, u, way).wait_recv()
                    value = value + inn[s - 1, lo:lo + n].astype(F32)
                out[s, lo:lo + n] = value.astype(BF16)
                hop(s, u, way).start()
    def window(sx):
        return pl.ds(pl.multiple_of(128 * sx, 128), 256)

    def r2(u, dx):
        px, part = wrap(x + dx, NX), pl.ds(*SUBS[u])
        return send(
            mine.at[part, window(px)], r2_in.at[x, part], r2_s.at[u, dx], r2_r.at[u, x], at_z(y, px, z, c)
        )

    def r3(u, sx):
        part = pl.ds(*SUBS[u])
        return send(
            r2_in.at[sx, part], r3_in.at[q, part], r3_s.at[u, sx], r3_r.at[u, q], at_z(y, x, home_z(sx), c)
        )

    def forward(u):
        lo, n = SUBS[u]
        for dx in (0, 1, 3, 2):
            sx = wrap(x + dx, NX)
            if dx:
                send(
                    mine.at[pl.ds(lo, n), pl.ds(0, 256)], r2_in.at[sx, pl.ds(lo, n)],
                    r2_s.at[u, dx], r2_r.at[u, sx], at_z(y, sx, z, c),
                ).wait_recv()

            @pl.when(home_z(sx) != z)
            def _():
                r3(u, sx).start()

            @pl.when(home_z(sx) == z)
            def _():
                r3_in[q, lo:lo + n] = r2_in[sx, lo:lo + n]

    for u, (lo, n) in enumerate(SUBS):
        value = block(y, (lo, n))
        hop(3, u, -1).wait_recv()
        value = value + left_in[3, lo:lo + n].astype(F32)
        hop(3, u, 1).wait_recv()
        mine[lo:lo + n] = (value + right_in[3, lo:lo + n].astype(F32)).astype(BF16)
        for dx in (1, 3, 2):
            r2(u, dx).start()
        r2_in[x, lo:lo + n] = mine[lo:lo + n, window(x)]
        if u:
            forward(u - 1)
    forward(len(SUBS) - 1)
    for u, (lo, n) in enumerate(SUBS):
        total = jnp.zeros((n, 256), F32)
        for sq in range(NQ):
            @pl.when(owner_z(sq) != z)
            def _():
                send(
                    r2_in.at[0, pl.ds(lo, n)], r3_in.at[sq, pl.ds(lo, n)],
                    r3_s.at[u, 0], r3_r.at[u, sq], at_z(y, x, owner_z(sq), c),
                ).wait_recv()
            total = total + r3_in[sq, lo:lo + n].astype(F32)
        total = pltpu.roll(total, lax.rem(256 - 32 * x, 256), 1)
        if u == 0:
            pos_out[...] = total[:, 0:160]
        else:
            acc[lo:lo + n, 0:256] = total
    dep_out[...] = acc[TAGS:K, 0:256].T[0:160]

    for sq in range(NQ):
        @pl.when(w_goes(sq))
        def _():
            for copy in w_send(sq):
                copy.wait_send()
    for i in range(len(PARTNERS)):
        meta_send(i).wait_send()
        for k in range(CHUNKS):
            for j in range(2):
                act_send(k, i, j).wait_send()
    for s in range(4):
        for way, steps in ((1, 4), (-1, 3)):
            if s < steps:
                ring(s, way).wait_send()
            for u in range(len(SUBS)):
                if s >= first(u, way):
                    hop(s, u, way).wait_send()
    for u in range(len(SUBS)):
        for dx in (1, 3, 2):
            r2(u, dx).wait_send()
        for sx in range(NX):
            @pl.when(home_z(sx) != z)
            def _():
                r3(u, sx).wait_send()


def local(activations, pos_weight, depth_weight, tags, depths, counts):
    acts = jnp.transpose(activations, (1, 0, 2)).reshape(SLOTS * 16, D)
    dma, vm = pltpu.SemaphoreType.DMA, pltpu.VMEM
    in_vmem = pl.BlockSpec(memory_space=vm)
    pos, dep = pl.pallas_call(
        kernel,
        out_shape=(jax.ShapeDtypeStruct((TAGS, 160), F32), jax.ShapeDtypeStruct((160, RANK), F32)),
        in_specs=[pl.BlockSpec(memory_space=pl.ANY)] + [in_vmem] * 5,
        out_specs=(in_vmem, in_vmem),
        scratch_shapes=[
            vm((CHUNKS, SLOTS * 16, WIDE), BF16), vm((CHUNKS, 16, PAD, WIDE), BF16), vm((GROUP, PAD, D), BF16),
            vm((TAGS, 256), F32), vm((TAGS, 256), BF16), vm((NX, TAGS, 256), BF16), vm((NX, 160, RANK), BF16),
            vm((NY, K, OWN), BF16),
            vm((2, 8, 128), F32), vm((GROUP, 8, 128), F32), vm((K, GROUP * PAD), F32), vm((K, GROUP * PAD), BF16),
            vm((4, K, OWN), BF16), vm((4, K, OWN), BF16), vm((4, K, OWN), BF16), vm((4, K, OWN), BF16),
            vm((K, OWN), BF16), vm((NX, K, 256), BF16), vm((NQ, K, 256), BF16),
            dma((CHUNKS,)), dma((CHUNKS, 15, 2)), dma((CHUNKS, GROUP, 2)),
            dma((NQ,)), dma((NX,)), dma((NQ,)), dma((NX,)),
            dma((4,)), dma((4,)), dma((3,)), dma((3,)), dma((15,)), dma((GROUP,)),
            dma((4, 4)), dma((4, 4)), dma((4, 4)), dma((4, 4)), dma((4, 4)), dma((4, NX)), dma((4, NX)), dma((4, NQ)),
        ],
        compiler_params=pltpu.CompilerParams(
            collective_id=0, has_side_effects=True, vmem_limit_bytes=61 * 1024 * 1024
        ),
    )(
        acts, pos_weight[0], depth_weight[0].T,
        tags.reshape(1, SLOTS), depths.reshape(1, SLOTS), counts.reshape(1, 1),
    )
    return pos[None], dep.T[None]


def solution(mesh):
    in_specs = (
        P(None, ("tok", "layer"), None),
        P("layer", None, "tok"),
        P("layer", None, "tok"),
        P(("tok", "layer")),
        P(("tok", "layer")),
        P(("tok", "layer")),
    )
    out_specs = (P("layer", None, "tok"), P("layer", None, "tok"))
    return jax.shard_map(local, mesh=mesh, in_specs=in_specs, out_specs=out_specs, check_vma=False)
```
